1024 devices in a mesh: dp: 16 (over z, core), ctx: 4 (over x_lo), tp: 16 (over y, x_hi).
Axes of the slice: x: 8 (x_hi: 2, x_lo: 4; x = x_hi * 4 + x_lo), y: 8, z: 8, core: 2. Of those that a mesh axis runs over, the one named last changes fastest.
Arguments:
- routed_experts: int32 [16384, 8], P(('dp', 'ctx', 'tp')), may hold values from 0 to 63, all different within a row; in each aligned block of 16 rows (0 to 15, 16 to 31, ...) at most 3 rows name the same one
- route_gates: float32 [16384, 8], P(('dp', 'ctx', 'tp')), may hold values from 0.03 to 0.4
- expert_hidden: bfloat16 [64, 16, 64, 3, 768], P(('ctx', 'tp'), 'dp'), may hold values from -6 to 6
- down_weight: bfloat16 [64, 768, 4096], P(('ctx', 'tp'), None, 'dp'), may hold values from -0.21875 to 0.21875
- output_grad: bfloat16 [16384, 4096], P(('dp', 'ctx', 'tp')), may hold values from -1.5 to 1.5
Outputs:
- combined: bfloat16 [16384, 4096], P(('dp', 'ctx', 'tp'))
- down_gradient: float32 [64, 768, 4096], P(('ctx', 'tp'), None, 'dp')
The draws below stay inside these ranges and needn't reach their ends.
Inputs may be any that keep to these rules, and one draw needn't show every extreme that they name: `routed_experts`: each row names 8 different experts. Among the routes of one device's 16 tokens (aligned blocks of rows) no expert is named more than 3 times, and in every draw some block names some expert exactly 3 times.
All inputs are finite; a program needn't handle non-finite values.
Results may differ from the reference program's by a relative error of at most 0.0049.
Values may be sent and summed in bfloat16 or wider, within the bound.
No kernel may reach another device: no remote copies, remote signals or barrier semaphores. Data moves between devices by JAX's collectives and lax.ppermute only.
A program may use at most 32 MiB of HBM per device.

```python
import math
import jax
import jax.numpy as jnp
import numpy as np
from jax import lax

D = 4096
FF = 768
TOPK = 8
TOK_OWN = 16
REPLICAS = 16
SOURCES = 64
EXPERTS = 64
CAP = 3
TOKENS = 16384
N_DP = 16


def levels(rng, dims, shards, smallest, largest):
    factor_of, own = 1.0, jax.random.fold_in(rng, 6)
    for position, shards_of in shards:
        steps = jnp.exp(jax.random.uniform(jax.random.fold_in(own, position), (shards_of,), jnp.float32, smallest / len(shards), largest / len(shards)))
        factor_of = factor_of * jnp.repeat(steps, dims[position] // shards_of).reshape([-1 if axis == position else 1 for axis in range(len(dims))])
    return factor_of


def routed_block(own_key, own, number, rows, number_of, top, bound, slope):
    ranking = jax.random.permutation(own_key, number_of)
    crowded, usual = load_shares(number_of, rows * top, bound, slope, True), load_shares(number_of, rows * top, bound, slope, False)
    places = jnp.arange(number_of)

    def named(sizes, rotation):
        used = int((sizes > 0).sum())
        fixed = max(1, used // 4)
        shifted = fixed + (places - fixed + rotation * (used - fixed)) % max(1, number_of - fixed)
        return jnp.zeros((number_of,), jnp.int32).at[ranking[jnp.where(places < fixed, places, shifted)]].set(jnp.asarray(sizes, jnp.int32))

    sizes = jnp.where(number % 4 == 0, named(crowded, number // 4), named(usual, number - number // 4 - 1))
    mixed = jax.random.permutation(jax.random.fold_in(own, 3), number_of)
    source_of, taker = mixed[0:number_of // 2 * 2:2], mixed[1:number_of // 2 * 2:2]
    room = jnp.minimum(sizes[source_of] - 1, bound - sizes[taker]) // 2
    room = jnp.where((source_of == ranking[0]) | (taker == ranking[0]) | (sizes[taker] == 0), 0, jnp.maximum(room, 0))
    shifted = jax.random.randint(jax.random.fold_in(own, 4), (number_of // 2,), 0, 1 << 20) % (room + 1)
    sizes = sizes.at[source_of].add(-shifted).at[taker].add(shifted)
    members = jnp.searchsorted(jnp.cumsum(sizes), jnp.arange(rows * top), side="right").astype(jnp.int32)
    grid = members.reshape(top, rows).T
    grid = grid[jax.random.permutation(jax.random.fold_in(own, 1), rows)]
    rotation = jax.random.randint(jax.random.fold_in(own, 2), (rows, 1), 0, top)
    return jnp.take_along_axis(grid, (jnp.arange(top)[None, :] + rotation) % top, axis=1)


def load_shares(amount, total, bound, lean, full):
    weights = [(1 << 20) // math.isqrt(grade ** lean) + 1 for grade in range(1, amount + 1)]
    largest = bound if full else min(bound, max(-(-total // amount), total * weights[0] // sum(weights)))
    least = 1 if total - largest >= amount - 1 else 0
    counts, spare = [largest] + [least] * (amount - 1), total - largest - least * (amount - 1)
    while spare > 0:
        free = [i for i in range(1, amount) if counts[i] < largest] or [i for i in range(1, amount) if counts[i] < bound]
        mass, budget = sum([weights[i] for i in free]), spare
        for i in free:
            extra = min(bound - counts[i], max(1, budget * weights[i] // mass), spare)
            counts[i] = counts[i] + extra
            spare = spare - extra
    return np.array(counts)


def noise(own_key, dims, width, most, pieces=(), held_as=jnp.bfloat16):
    drawn = width * jax.random.normal(own_key, dims, jnp.float32)
    if pieces:
        drawn = drawn * levels(own_key, dims, pieces, -0.22, 0.18)
    return jnp.clip(drawn, -most, most).astype(held_as)


def setup_inputs(seed: int = 0) -> dict:
    splits = jax.random.split(jax.random.key(seed), 6)
    routed_experts_keys = jax.random.split(jax.random.fold_in(splits[0], 1), TOKENS // TOK_OWN)
    routed_experts_turns = jax.random.permutation(jax.random.fold_in(splits[0], 3), TOKENS // TOK_OWN)
    routed_experts = jax.vmap(lambda own, number: routed_block(jax.random.fold_in(splits[0], 2), own, number, TOK_OWN, EXPERTS, TOPK, CAP, 2))(routed_experts_keys, routed_experts_turns).reshape((TOKENS, TOPK))
    route_gates = jnp.clip(jnp.exp(math.log(0.4) - 2.5902672 * jax.random.uniform(splits[1], (TOKENS, TOPK), jnp.float32) ** levels(splits[1], (TOKENS, TOPK), ((0, 1024),), -0.2, 0.2)), 0.03, 0.4)
    expert_hidden = noise(splits[2], (EXPERTS, REPLICAS, SOURCES, CAP, FF), 1.0, 6.0, ((0, 64), (1, 16)))
    down_weight = noise(splits[3], (EXPERTS, FF, D), FF ** -0.5, 0.21875, ((0, 64), (2, 16)))
    output_grad = noise(splits[4], (TOKENS, D), 0.25, 1.5, ((0, 1024),))
    return dict(routed_experts=routed_experts, route_gates=route_gates, expert_hidden=expert_hidden, down_weight=down_weight, output_grad=output_grad)


def slot_table(routed_experts):
    routes = TOK_OWN * TOPK
    flat_experts = routed_experts.reshape(N_DP * SOURCES, routes)
    same = flat_experts[:, :, None] == flat_experts[:, None, :]
    order = jnp.arange(routes, dtype=jnp.int32)
    before = order[None, :] < order[:, None]
    ranks = jnp.sum(jnp.logical_and(same, before[None]), axis=2).astype(jnp.int32)
    return flat_experts, ranks


def reference(routed_experts, route_gates, expert_hidden, down_weight, output_grad):
    routes = TOK_OWN * TOPK
    rows_per = N_DP * SOURCES * CAP
    flat_experts, ranks = slot_table(routed_experts)
    device = jnp.arange(N_DP * SOURCES, dtype=jnp.int32)
    slots = device[:, None] * CAP + ranks
    whole = (flat_experts * rows_per + slots).reshape(-1)
    token = (device[:, None] * TOK_OWN + jnp.arange(routes, dtype=jnp.int32)[None, :] // TOPK).reshape(-1)
    slot_token = jnp.full((EXPERTS * rows_per,), TOKENS, jnp.int32).at[whole].set(token).reshape(EXPERTS, rows_per)
    slot_gate = jnp.zeros((EXPERTS * rows_per,), jnp.float32).at[whole].set(route_gates.reshape(-1)).reshape(EXPERTS, rows_per)
    padded_grad = jnp.concatenate([output_grad, jnp.zeros((1, D), output_grad.dtype)], axis=0)

    def one_expert(mixed, items):
        hidden_block, weight_block, token_block, gate_block = items
        rows = hidden_block.reshape(rows_per, FF)
        produced = jnp.dot(rows, weight_block, preferred_element_type=jnp.float32).astype(jnp.bfloat16)
        mixed = mixed.at[token_block].add(gate_block[:, None] * produced.astype(jnp.float32), mode="drop")
        scaled = (gate_block[:, None] * padded_grad[token_block].astype(jnp.float32)).astype(jnp.bfloat16)
        gradient = jnp.dot(rows.T, scaled, preferred_element_type=jnp.float32)
        return mixed, gradient

    mixed, gradients = lax.scan(one_expert, jnp.zeros((TOKENS, D), jnp.float32), (expert_hidden, down_weight, slot_token, slot_gate))
    return mixed.astype(jnp.bfloat16), gradients
```

```python
import jax
import jax.numpy as jnp
from jax import lax
from jax.sharding import PartitionSpec as P

CORES = 2
LANES = 128
F32 = jnp.float32
BF16 = jnp.bfloat16


def expert_move(buffer):
    return lax.all_to_all(buffer, ("ctx", "tp"), split_axis=0, concat_axis=0, tiled=True)


def parts_of(values):
    high = values.astype(BF16)
    low = (values - high.astype(F32)).astype(BF16)
    return high, low


def three_parts(values):
    high, low = parts_of(values)
    last = (values - high.astype(F32) - low.astype(F32)).astype(BF16)
    return high, low, last


def body(routed_experts, route_gates, expert_hidden, down_weight, output_grad):
    dp = lax.axis_size("dp")
    chips = dp // CORES
    experts = lax.axis_size("ctx") * lax.axis_size("tp")
    own, topk = routed_experts.shape
    capacity, depth = expert_hidden.shape[3:]
    width = output_grad.shape[1]
    half = width // dp
    part = half * CORES
    tokens = chips * own
    column = [[z * CORES + c for z in range(chips)] for c in range(CORES)]
    swap = [(d, d ^ 1) for d in range(dp)]
    core = lax.axis_index("dp") & 1

    def chip_move(blocks):
        return lax.all_to_all(
            blocks, "dp", split_axis=0, concat_axis=0, tiled=True, axis_index_groups=column
        )

    rows = jnp.swapaxes(expert_hidden[0, 0], 0, 1).reshape(capacity * experts, depth)
    gathered = lax.all_gather(rows, "dp", axis=0, tiled=False, axis_index_groups=column)
    weight = down_weight[0]
    other = lax.ppermute(weight, "dp", swap)
    weight = jnp.concatenate(
        [jnp.where(core == 0, weight, other), jnp.where(core == 0, other, weight)], axis=1
    )

    table = jnp.concatenate(
        [routed_experts.astype(F32).astype(BF16), *three_parts(route_gates)], axis=1
    )
    table = jnp.pad(table, ((0, 0), (0, LANES - table.shape[1])))
    blocks = jnp.swapaxes(output_grad.reshape(own, chips, part), 0, 1)
    blocks = jnp.concatenate([blocks, jnp.broadcast_to(table, (chips, own, LANES))], axis=2)
    arrived = chip_move(blocks)
    grads = arrived[:, :, :part].reshape(tokens, part)
    table = arrived[:, :, part:].reshape(tokens, LANES).astype(F32)
    named = table[:, :topk]
    gates = sum(table[:, topk * i : topk * (i + 1)] for i in (1, 2, 3))

    ids = lax.broadcasted_iota(jnp.int32, (experts, tokens), 0).astype(F32)
    hit = named.T[:, None, :] == ids[None]
    names = jnp.any(hit, axis=0)
    gate_of = jnp.sum(jnp.where(hit, gates.T[:, None, :], 0.0), axis=0)
    at = lax.broadcasted_iota(jnp.int32, (tokens, tokens), 0)
    to = lax.broadcasted_iota(jnp.int32, (tokens, tokens), 1)
    earlier = jnp.logical_and(at // own == to // own, at < to).astype(BF16)
    rank = jnp.dot(names.astype(BF16), earlier, preferred_element_type=F32)
    replica = (lax.broadcasted_iota(jnp.int32, (experts, tokens), 1) // own).astype(F32)
    code = jnp.where(names, replica * capacity + rank, -1.0)
    lines = capacity * chips
    place = code[:, None, :] == lax.broadcasted_iota(jnp.int32, (1, lines, tokens), 1).astype(F32)
    placer = jnp.concatenate(
        [jnp.where(place, p.astype(F32)[:, None, :], 0.0).astype(BF16) for p in parts_of(gate_of)],
        axis=2,
    ).reshape(experts * lines, 2 * tokens)

    outgoing = jnp.dot(placer, jnp.concatenate([grads, grads], axis=0), preferred_element_type=F32)
    grad_rows = expert_move(outgoing.astype(BF16).reshape(experts, lines, part))

    hidden = gathered.reshape(lines * experts, depth)
    produced = jnp.dot(hidden, weight, preferred_element_type=F32).astype(BF16)
    returned = expert_move(jnp.swapaxes(produced.reshape(lines, experts, part), 0, 1))

    grad_rows = jnp.swapaxes(grad_rows, 0, 1).reshape(lines * experts, part)
    gradient = lax.dot_general(
        hidden, grad_rows, (((0,), (0,)), ((), ())), preferred_element_type=F32
    )
    kept = lax.dynamic_slice_in_dim(gradient, core * half, half, 1)
    gradient = kept + lax.ppermute(
        lax.dynamic_slice_in_dim(gradient, (1 - core) * half, half, 1), "dp", swap
    )

    mixed = lax.dot_general(
        placer,
        returned.reshape(experts * lines, part),
        (((0,), (0,)), ((), ())),
        preferred_element_type=F32,
    )
    mixed = (mixed[:tokens] + mixed[tokens:]).astype(BF16).reshape(chips, own, part)
    combined = jnp.swapaxes(chip_move(mixed), 0, 1).reshape(own, width)
    return (combined, gradient[None])


def solution(mesh):
    in_specs = (
        P(("dp", "ctx", "tp"), None),
        P(("dp", "ctx", "tp"), None),
        P(("ctx", "tp"), "dp", None, None, None),
        P(("ctx", "tp"), None, "dp"),
        P(("dp", "ctx", "tp"), None),
    )
    out_specs = (P(("dp", "ctx", "tp"), None), P(("ctx", "tp"), None, "dp"))
    return jax.shard_map(body, mesh=mesh, in_specs=in_specs, out_specs=out_specs, check_vma=False)
```

```python
import jax
import jax.numpy as jnp
from jax import lax
from jax.experimental.layout import Layout, with_layout_constraint
from jax.sharding import PartitionSpec as P

CORES = 2
LANES = 128
F32 = jnp.float32
BF16 = jnp.bfloat16


def expert_move(buffer):
    return lax.all_to_all(buffer, ("ctx", "tp"), split_axis=0, concat_axis=0, tiled=True)


def parts_of(values, count):
    parts = []
    for _ in range(count):
        part = lax.reduce_precision(values, 8, 7)
        parts.append(part.astype(BF16))
        values = values - part
    return parts


def placer_of(named, gates, experts, own, capacity, place_of):
    tokens = named.shape[0]
    groups = tokens // own
    shape = (experts, tokens)
    ids = lax.broadcasted_iota(jnp.int32, shape, 0).astype(F32)
    hit = named.T[:, None, :] == ids[None]
    names = jnp.any(hit, axis=0)
    gate_of = jnp.sum(jnp.where(hit, gates.T[:, None, :], 0.0), axis=0)
    at = lax.broadcasted_iota(jnp.int32, (tokens, tokens), 0)
    to = lax.broadcasted_iota(jnp.int32, (tokens, tokens), 1)
    earlier = jnp.logical_and(at // own == to // own, at < to).astype(BF16)
    rank = jnp.dot(names.astype(BF16), earlier, preferred_element_type=F32)
    group = place_of(lax.broadcasted_iota(jnp.int32, shape, 1) // own)
    code = jnp.where(names, group.astype(F32) * capacity + rank, -1.0)
    lines = capacity * groups
    place = code[:, None, :] == lax.broadcasted_iota(jnp.int32, (1, lines, tokens), 1).astype(F32)
    return jnp.concatenate(
        [jnp.where(place, p[:, None, :], jnp.zeros((), BF16)) for p in parts_of(gate_of, 2)], axis=2
    ).reshape(experts * lines, 2 * tokens)


def body(routed_experts, route_gates, expert_hidden, down_weight, output_grad):
    dp = lax.axis_size("dp")
    chips = dp // CORES
    experts = lax.axis_size("ctx") * lax.axis_size("tp")
    own, topk = routed_experts.shape
    capacity, depth = expert_hidden.shape[3:]
    width = output_grad.shape[1]
    half = width // dp
    part = half * CORES
    tokens = chips * own
    lines = chips * capacity
    held = capacity * experts
    column = [[z * CORES + c for z in range(chips)] for c in range(CORES)]
    swap = [(d, d ^ 1) for d in range(dp)]
    core = lax.axis_index("dp") & 1
    chip = lax.axis_index("dp") // CORES

    def shift(block, by):
        moved = lax.ppermute(block, "dp", [(d, (d + CORES * by) % dp) for d in range(dp)])
        return with_layout_constraint(moved, Layout((0, 1)))

    def chip_move(blocks):
        return lax.all_to_all(
            blocks, "dp", split_axis=0, concat_axis=0, tiled=True, axis_index_groups=column
        )

    def along(group):
        return (group + chips - chip) % chips

    def in_order(group):
        ahead = along(group)
        return jnp.where(
            ahead > chips // 2, 2 * (chips - ahead), jnp.maximum(2 * ahead - 1, 0)
        )

    named = routed_experts.astype(F32)
    blocks = jnp.swapaxes(output_grad.reshape(own, chips, part), 0, 1).reshape(tokens, part)
    placer = placer_of(
        jnp.tile(named, (chips, 1)), jnp.tile(route_gates, (chips, 1)), experts, own, capacity, along
    )
    outgoing = jnp.dot(placer, jnp.concatenate([blocks, blocks], axis=0), preferred_element_type=F32)
    outgoing = outgoing.astype(BF16).reshape(experts, lines, part)

    table = jnp.concatenate([named.astype(BF16), *parts_of(route_gates, 3)], axis=1)
    table = jnp.pad(table, ((0, 0), (0, depth - table.shape[1])))
    rows = jnp.swapaxes(expert_hidden[0, 0], 0, 1).reshape(held, depth)
    mine = with_layout_constraint(jnp.concatenate([rows, table], axis=0), Layout((0, 1)))
    order = [0]
    up = down = mine
    around = [mine]
    for step in range(1, chips // 2):
        up, down = shift(up, 1), shift(down, -1)
        if step == 1:
            up, down, _ = lax.optimization_barrier((up, down, outgoing))
        order += [step, chips - step]
        around += [down, up]
    middle = mine.shape[0] // 2
    order.append(chips // 2)
    around.append(jnp.concatenate([shift(up[:middle], 1), shift(down[middle:], -1)], axis=0))

    scaled = jnp.swapaxes(expert_move(outgoing), 0, 1)
    scaled = scaled.reshape(chips, held, part)

    weight = down_weight[0]
    other = lax.ppermute(weight, "dp", swap)
    weight = jnp.concatenate(
        [jnp.where(core == 0, weight, other), jnp.where(core == 0, other, weight)], axis=1
    )
    weight = lax.optimization_barrier(weight)
    early = chips // 2 + 1
    hidden = [
        jnp.concatenate([block[:held] for block in blocks], axis=0)
        for blocks in (around[:early], around[early:])
    ]
    produced = [jnp.dot(h, weight, preferred_element_type=F32).astype(BF16) for h in hidden]
    produced = jnp.concatenate([p.reshape(-1, experts, part) for p in produced], axis=0)
    tables = jnp.concatenate([block[held:, :LANES] for block in around], axis=0)
    produced, scaled, tables = lax.optimization_barrier(
        (jnp.swapaxes(produced, 0, 1), scaled, tables)
    )
    returned = expert_move(produced)

    wanted = lax.broadcasted_iota(jnp.int32, (tokens, tokens), 0)
    source = in_order(wanted // own) * own + wanted % own
    turn = (source == lax.broadcasted_iota(jnp.int32, (tokens, tokens), 1)).astype(BF16)
    tables = jnp.dot(turn, tables, preferred_element_type=F32)
    gates = sum(tables[:, topk * i : topk * (i + 1)] for i in (1, 2, 3))
    mixer = placer_of(tables[:, :topk], gates, experts, own, capacity, in_order)
    mixed = lax.dot_general(
        mixer,
        returned.reshape(experts * lines, part),
        (((0,), (0,)), ((), ())),
        preferred_element_type=F32,
    )
    mixed = (mixed[:tokens] + mixed[tokens:]).astype(BF16).reshape(chips, own, part)
    combined = jnp.swapaxes(chip_move(mixed), 0, 1).reshape(own, width)

    grad_rows = [scaled[0]] + [shift(scaled[(chips - i) % chips], -i) for i in order[1:]]
    gradient = sum(
        lax.dot_general(
            h, jnp.concatenate(g, axis=0), (((0,), (0,)), ((), ())), preferred_element_type=F32
        )
        for h, g in zip(hidden, (grad_rows[:early], grad_rows[early:]))
    )
    kept = lax.dynamic_slice_in_dim(gradient, core * half, half, 1)
    gradient = kept + lax.ppermute(
        lax.dynamic_slice_in_dim(gradient, (1 - core) * half, half, 1), "dp", swap
    )
    return (combined, gradient[None])


def solution(mesh):
    in_specs = (
        P(("dp", "ctx", "tp"), None),
        P(("dp", "ctx", "tp"), None),
        P(("ctx", "tp"), "dp", None, None, None),
        P(("ctx", "tp"), None, "dp"),
        P(("dp", "ctx", "tp"), None),
    )
    out_specs = (P(("dp", "ctx", "tp"), None), P(("ctx", "tp"), None, "dp"))
    return jax.shard_map(body, mesh=mesh, in_specs=in_specs, out_specs=out_specs, check_vma=False)
```

```python
import jax
import jax.numpy as jnp
from jax import lax
from jax.experimental.layout import Layout, with_layout_constraint
from jax.sharding import PartitionSpec as P


CORES = 2
LANES = 128
F32 = jnp.float32
BF16 = jnp.bfloat16


def expert_move(buffer):
    return lax.all_to_all(buffer, ("ctx", "tp"), split_axis=0, concat_axis=0, tiled=True)


def parts_of(values, count):
    parts = []
    for _ in range(count):
        part = lax.reduce_precision(values, 8, 7)
        parts.append(part.astype(BF16))
        values = values - part
    return parts


def placer_of(named, gates, experts, own, capacity, place_of):
    tokens = named.shape[0]
    groups = tokens // own
    shape = (experts, tokens)
    ids = lax.broadcasted_iota(jnp.int32, shape, 0).astype(F32)
    hit = named.T[:, None, :] == ids[None]
    names = jnp.any(hit, axis=0)
    gate_of = jnp.sum(jnp.where(hit, gates.T[:, None, :], 0.0), axis=0)
    at = lax.broadcasted_iota(jnp.int32, (tokens, tokens), 0)
    to = lax.broadcasted_iota(jnp.int32, (tokens, tokens), 1)
    earlier = jnp.logical_and(at // own == to // own, at < to).astype(BF16)
    rank = jnp.dot(names.astype(BF16), earlier, preferred_element_type=F32)
    group = place_of(lax.broadcasted_iota(jnp.int32, shape, 1) // own)
    code = jnp.where(names, group.astype(F32) * capacity + rank, -1.0)
    lines = capacity * groups
    place = code[:, None, :] == lax.broadcasted_iota(jnp.int32, (1, lines, tokens), 1).astype(F32)
    return jnp.concatenate(
        [jnp.where(place, p[:, None, :], jnp.zeros((), BF16)) for p in parts_of(gate_of, 2)], axis=2
    ).reshape(experts * lines, 2 * tokens)


def layer(routed_experts, route_gates, expert_hidden, down_weight, output_grad):
    dp = lax.axis_size("dp")
    chips = dp // CORES
    experts = lax.axis_size("ctx") * lax.axis_size("tp")
    own, topk = routed_experts.shape
    capacity, depth = expert_hidden.shape[3:]
    width = output_grad.shape[1]
    half = width // dp
    part = half * CORES
    tokens = chips * own
    lines = chips * capacity
    held = capacity * experts
    column = [[z * CORES + c for z in range(chips)] for c in range(CORES)]
    swap = [(d, d ^ 1) for d in range(dp)]
    core = lax.axis_index("dp") & 1
    chip = lax.axis_index("dp") // CORES

    def shift(block, by):
        moved = lax.ppermute(block, "dp", [(d, (d + CORES * by) % dp) for d in range(dp)])
        return with_layout_constraint(moved, Layout((0, 1)))

    def chip_move(blocks):
        return lax.all_to_all(
            blocks, "dp", split_axis=0, concat_axis=0, tiled=True, axis_index_groups=column
        )

    def along(group):
        return (group + chips - chip) % chips

    def in_order(group):
        ahead = along(group)
        return jnp.where(
            ahead > chips // 2, 2 * (chips - ahead), jnp.maximum(2 * ahead - 1, 0)
        )

    named = routed_experts.astype(F32)

    blocks = jnp.swapaxes(output_grad.reshape(own, chips, part), 0, 1).reshape(tokens, part)
    placer = placer_of(
        jnp.tile(named, (chips, 1)), jnp.tile(route_gates, (chips, 1)), experts, own, capacity, along
    )
    outgoing = jnp.dot(placer, jnp.concatenate([blocks, blocks], axis=0), preferred_element_type=F32)
    outgoing = outgoing.astype(BF16).reshape(experts, lines, part)

    table = jnp.concatenate([named.astype(BF16), *parts_of(route_gates, 3)], axis=1)
    table = jnp.pad(table, ((0, 0), (0, depth - table.shape[1])))
    rows = jnp.swapaxes(expert_hidden[0, 0], 0, 1).reshape(held, depth)
    mine = with_layout_constraint(jnp.concatenate([rows, table], axis=0), Layout((0, 1)))
    order = [0]
    up = down = mine
    around = [mine]
    for step in range(1, chips // 2):
        up, down = shift(up, 1), shift(down, -1)
        order += [step, chips - step]
        around += [down, up]
    middle = mine.shape[0] // 2
    order.append(chips // 2)
    around.append(jnp.concatenate([shift(up[:middle], 1), shift(down[middle:], -1)], axis=0))

    scaled = expert_move(outgoing)
    scaled = jnp.swapaxes(scaled, 0, 1)
    scaled = scaled.reshape(chips, held, part)

    weight = down_weight[0]
    other = lax.ppermute(weight, "dp", swap)
    weight = jnp.concatenate(
        [jnp.where(core == 0, weight, other), jnp.where(core == 0, other, weight)], axis=1
    )
    weight = lax.optimization_barrier(weight)
    early = chips // 2 + 1
    hidden = [
        jnp.concatenate([block[:held] for block in blocks], axis=0)
        for blocks in (around[:early], around[early:])
    ]
    produced = [jnp.dot(h, weight, preferred_element_type=F32).astype(BF16) for h in hidden]
    produced = jnp.concatenate([p.reshape(-1, experts, part) for p in produced], axis=0)
    tables = jnp.concatenate([block[held:, :LANES] for block in around], axis=0)
    produced, scaled, tables = lax.optimization_barrier(
        (jnp.swapaxes(produced, 0, 1), scaled, tables)
    )
    returned = expert_move(produced)

    wanted = lax.broadcasted_iota(jnp.int32, (tokens, tokens), 0)
    source = in_order(wanted // own) * own + wanted % own
    turn = (source == lax.broadcasted_iota(jnp.int32, (tokens, tokens), 1)).astype(BF16)
    tables = jnp.dot(turn, tables, preferred_element_type=F32)
    gates = sum(tables[:, topk * i : topk * (i + 1)] for i in (1, 2, 3))
    mixer = placer_of(tables[:, :topk], gates, experts, own, capacity, in_order)
    mixed = lax.dot_general(
        mixer,
        returned.reshape(experts * lines, part),
        (((0,), (0,)), ((), ())),
        preferred_element_type=F32,
    )
    mixed = (mixed[:tokens] + mixed[tokens:]).astype(BF16).reshape(chips, own, part)
    combined = chip_move(mixed)
    combined = jnp.swapaxes(combined, 0, 1).reshape(own, width)

    grad_rows = [scaled[0]] + [shift(scaled[(chips - i) % chips], -i) for i in order[1:]]
    hidden, _ = lax.optimization_barrier((hidden, mixed))
    gradient = sum(
        lax.dot_general(
            h, jnp.concatenate(g, axis=0), (((0,), (0,)), ((), ())), preferred_element_type=F32
        )
        for h, g in zip(hidden, (grad_rows[:early], grad_rows[early:]))
    )
    kept = lax.dynamic_slice_in_dim(gradient, core * half, half, 1)
    given = lax.dynamic_slice_in_dim(gradient, (1 - core) * half, half, 1)
    gradient = kept + lax.ppermute(given, "dp", swap)
    return (combined, gradient[None])


def solution(mesh):
    in_specs = (
        P(("dp", "ctx", "tp"), None),
        P(("dp", "ctx", "tp"), None),
        P(("ctx", "tp"), "dp", None, None, None),
        P(("ctx", "tp"), None, "dp"),
        P(("dp", "ctx", "tp"), None),
    )
    out_specs = (P(("dp", "ctx", "tp"), None), P(("ctx", "tp"), None, "dp"))
    return jax.shard_map(layer, mesh=mesh, in_specs=in_specs, out_specs=out_specs, check_vma=False)
```

```python
import jax
import jax.numpy as jnp
from jax import lax
from jax.experimental.layout import Layout, with_layout_constraint
from jax.sharding import PartitionSpec as P


CORES = 2
LANES = 128
F32 = jnp.float32
BF16 = jnp.bfloat16


def expert_move(buffer):
    return lax.all_to_all(buffer, ("ctx", "tp"), split_axis=0, concat_axis=0, tiled=True)


def parts_of(values, count):
    parts = []
    for _ in range(count):
        part = lax.reduce_precision(values, 8, 7)
        parts.append(part.astype(BF16))
        values = values - part
    return parts


def placer_of(named, gates, experts, own, capacity, place_of):
    tokens = named.shape[0]
    groups = tokens // own
    shape = (experts, tokens)
    ids = lax.broadcasted_iota(jnp.int32, shape, 0).astype(F32)
    hit = named.T[:, None, :] == ids[None]
    names = jnp.any(hit, axis=0)
    gate_of = jnp.sum(jnp.where(hit, gates.T[:, None, :], 0.0), axis=0)
    at = lax.broadcasted_iota(jnp.int32, (tokens, tokens), 0)
    to = lax.broadcasted_iota(jnp.int32, (tokens, tokens), 1)
    earlier = jnp.logical_and(at // own == to // own, at < to).astype(BF16)
    rank = jnp.dot(names.astype(BF16), earlier, preferred_element_type=F32)
    group = place_of(lax.broadcasted_iota(jnp.int32, shape, 1) // own)
    code = jnp.where(names, group.astype(F32) * capacity + rank, -1.0)
    lines = capacity * groups
    place = code[:, None, :] == lax.broadcasted_iota(jnp.int32, (1, lines, tokens), 1).astype(F32)
    return jnp.concatenate(
        [jnp.where(place, p[:, None, :], jnp.zeros((), BF16)) for p in parts_of(gate_of, 2)], axis=2
    ).reshape(experts * lines, 2 * tokens)


def layer(routed_experts, route_gates, expert_hidden, down_weight, output_grad):
    dp = lax.axis_size("dp")
    chips = dp // CORES
    experts = lax.axis_size("ctx") * lax.axis_size("tp")
    own, topk = routed_experts.shape
    capacity, depth = expert_hidden.shape[3:]
    width = output_grad.shape[1]
    half = width // dp
    part = half * CORES
    tokens = chips * own
    lines = chips * capacity
    held = capacity * experts
    column = [[z * CORES + c for z in range(chips)] for c in range(CORES)]
    swap = [(d, d ^ 1) for d in range(dp)]
    core = lax.axis_index("dp") & 1
    chip = lax.axis_index("dp") // CORES

    def shift(block, by):
        moved = lax.ppermute(block, "dp", [(d, (d + CORES * by) % dp) for d in range(dp)])
        return with_layout_constraint(moved, Layout((0, 1)))

    def chip_move(blocks):
        return lax.all_to_all(
            blocks, "dp", split_axis=0, concat_axis=0, tiled=True, axis_index_groups=column
        )

    def in_order(group):
        ahead = (group + chips - chip) % chips
        return jnp.where(
            ahead > chips // 2, 2 * (chips - ahead), jnp.maximum(2 * ahead - 1, 0)
        )

    table = jnp.concatenate(
        [routed_experts.astype(F32).astype(BF16), *parts_of(route_gates, 3)], axis=1
    )
    table = jnp.pad(table, ((0, 0), (0, LANES - table.shape[1])))
    blocks = jnp.swapaxes(output_grad.reshape(own, chips, part), 0, 1)
    blocks = jnp.concatenate([blocks, jnp.broadcast_to(table, (chips, own, LANES))], axis=2)
    arrived = chip_move(blocks)
    grads = arrived[:, :, :part].reshape(tokens, part)
    tables = arrived[:, :, part:].reshape(tokens, LANES).astype(F32)
    gates = sum(tables[:, topk * i : topk * (i + 1)] for i in (1, 2, 3))
    placer = placer_of(tables[:, :topk], gates, experts, own, capacity, in_order)
    outgoing = jnp.dot(placer, jnp.concatenate([grads, grads], axis=0), preferred_element_type=F32)
    outgoing = outgoing.astype(BF16).reshape(experts, lines, part)
    scaled = expert_move(outgoing)

    mine = jnp.swapaxes(expert_hidden[0, 0], 0, 1).reshape(held, depth)
    up = down = mine
    around = [mine]
    for _ in range(1, chips // 2):
        up, down = shift(up, 1), shift(down, -1)
        around += [down, up]
    middle = held // 2
    around.append(jnp.concatenate([shift(up[:middle], 1), shift(down[middle:], -1)], axis=0))

    weight = down_weight[0]
    other = lax.ppermute(weight, "dp", swap)
    weight = jnp.concatenate(
        [jnp.where(core == 0, weight, other), jnp.where(core == 0, other, weight)], axis=1
    )
    weight = lax.optimization_barrier(weight)
    early = chips // 2 + 1
    hidden = [
        jnp.concatenate(blocks, axis=0)
        for blocks in (around[:early], around[early:])
    ]
    produced = [jnp.dot(h, weight, preferred_element_type=F32).astype(BF16) for h in hidden]
    produced = jnp.concatenate([p.reshape(-1, experts, part) for p in produced], axis=0)
    returned = expert_move(jnp.swapaxes(produced, 0, 1))

    mixed = lax.dot_general(
        placer,
        returned.reshape(experts * lines, part),
        (((0,), (0,)), ((), ())),
        preferred_element_type=F32,
    )
    mixed = (mixed[:tokens] + mixed[tokens:]).astype(BF16).reshape(chips, own, part)
    combined = chip_move(mixed)
    combined = jnp.swapaxes(combined, 0, 1).reshape(own, width)

    grad_rows = jnp.swapaxes(scaled, 0, 1).reshape(lines * experts, part)
    cut = early * held
    gradient = sum(
        lax.dot_general(h, g, (((0,), (0,)), ((), ())), preferred_element_type=F32)
        for h, g in zip(hidden, (grad_rows[:cut], grad_rows[cut:]))
    )
    kept = lax.dynamic_slice_in_dim(gradient, core * half, half, 1)
    given = lax.dynamic_slice_in_dim(gradient, (1 - core) * half, half, 1)
    gradient = kept + lax.ppermute(given, "dp", swap)
    return (combined, gradient[None])


def solution(mesh):
    in_specs = (
        P(("dp", "ctx", "tp"), None),
        P(("dp", "ctx", "tp"), None),
        P(("ctx", "tp"), "dp", None, None, None),
        P(("ctx", "tp"), None, "dp"),
        P(("dp", "ctx", "tp"), None),
    )
    out_specs = (P(("dp", "ctx", "tp"), None), P(("ctx", "tp"), None, "dp"))
    return jax.shard_map(layer, mesh=mesh, in_specs=in_specs, out_specs=out_specs, check_vma=False)
```

```python
import jax
import jax.numpy as jnp
from jax import lax
from jax.experimental.layout import Layout, with_layout_constraint
from jax.sharding import PartitionSpec as P


CORES = 2
LANES = 128
F32 = jnp.float32
BF16 = jnp.bfloat16


def expert_move(buffer):
    return lax.all_to_all(buffer, ("ctx", "tp"), split_axis=0, concat_axis=0, tiled=True)


def parts_of(values, count):
    parts = []
    for _ in range(count):
        part = lax.reduce_precision(values, 8, 7)
        parts.append(part.astype(BF16))
        values = values - part
    return parts


def placer_of(named, gates, experts, own, capacity, place_of):
    tokens = named.shape[0]
    groups = tokens // own
    shape = (experts, tokens)
    ids = lax.broadcasted_iota(jnp.int32, shape, 0).astype(F32)
    hit = named.T[:, None, :] == ids[None]
    names = jnp.any(hit, axis=0)
    gate_of = jnp.sum(jnp.where(hit, gates.T[:, None, :], 0.0), axis=0)
    at = lax.broadcasted_iota(jnp.int32, (tokens, tokens), 0)
    to = lax.broadcasted_iota(jnp.int32, (tokens, tokens), 1)
    earlier = jnp.logical_and(at // own == to // own, at < to).astype(BF16)
    rank = jnp.dot(names.astype(BF16), earlier, preferred_element_type=F32)
    group = place_of(lax.broadcasted_iota(jnp.int32, shape, 1) // own)
    code = jnp.where(names, group.astype(F32) * capacity + rank, -1.0)
    lines = capacity * groups
    place = code[:, None, :] == lax.broadcasted_iota(jnp.int32, (1, lines, tokens), 1).astype(F32)
    return jnp.concatenate(
        [jnp.where(place, p[:, None, :], jnp.zeros((), BF16)) for p in parts_of(gate_of, 2)], axis=2
    ).reshape(experts * lines, 2 * tokens)


def layer(routed_experts, route_gates, expert_hidden, down_weight, output_grad):
    dp = lax.axis_size("dp")
    chips = dp // CORES
    experts = lax.axis_size("ctx") * lax.axis_size("tp")
    own, topk = routed_experts.shape
    capacity, depth = expert_hidden.shape[3:]
    width = output_grad.shape[1]
    half = width // dp
    part = half * CORES
    tokens = chips * own
    lines = chips * capacity
    held = capacity * experts
    column = [[z * CORES + c for z in range(chips)] for c in range(CORES)]
    swap = [(d, d ^ 1) for d in range(dp)]
    core = lax.axis_index("dp") & 1
    chip = lax.axis_index("dp") // CORES

    def shift(block, by):
        moved = lax.ppermute(block, "dp", [(d, (d + CORES * by) % dp) for d in range(dp)])
        return with_layout_constraint(moved, Layout((0, 1)))

    def chip_move(blocks):
        return lax.all_to_all(
            blocks, "dp", split_axis=0, concat_axis=0, tiled=True, axis_index_groups=column
        )

    def in_order(group):
        ahead = (group + chips - chip) % chips
        return jnp.where(
            ahead > chips // 2, 2 * (chips - ahead), jnp.maximum(2 * ahead - 1, 0)
        )

    table = jnp.concatenate(
        [routed_experts.astype(F32).astype(BF16), *parts_of(route_gates, 3)], axis=1
    )
    table = jnp.pad(table, ((0, 0), (0, LANES - table.shape[1])))
    blocks = jnp.swapaxes(output_grad.reshape(own, chips, part), 0, 1)
    blocks = jnp.concatenate([blocks, jnp.broadcast_to(table, (chips, own, LANES))], axis=2)
    arrived = chip_move(blocks)
    grads = arrived[:, :, :part].reshape(tokens, part)
    tables = arrived[:, :, part:].reshape(tokens, LANES).astype(F32)
    gates = sum(tables[:, topk * i : topk * (i + 1)] for i in (1, 2, 3))
    placer = placer_of(tables[:, :topk], gates, experts, own, capacity, in_order)
    outgoing = jnp.dot(placer, jnp.concatenate([grads, grads], axis=0), preferred_element_type=F32)
    outgoing = outgoing.astype(BF16).reshape(experts, lines, part)
    scaled = expert_move(outgoing)

    mine = jnp.swapaxes(expert_hidden[0, 0], 0, 1).reshape(held, depth)
    up = down = mine
    around = [mine]
    for _ in range(1, chips // 2):
        up, down = shift(up, 1), shift(down, -1)
        around += [down, up]
    last = [(d, (d + (CORES if d % CORES == 0 else -CORES)) % dp) for d in range(dp)]
    far = lax.ppermute(jnp.where(core == 0, up, down), "dp", last)
    around.append(with_layout_constraint(far, Layout((0, 1))))

    weight = down_weight[0]
    other = lax.ppermute(weight, "dp", swap)
    weight = jnp.concatenate(
        [jnp.where(core == 0, weight, other), jnp.where(core == 0, other, weight)], axis=1
    )
    weight = lax.optimization_barrier(weight)
    early = chips // 2 + 1
    hidden = [
        jnp.concatenate(blocks, axis=0)
        for blocks in (around[:early], around[early:])
    ]
    produced = [jnp.dot(h, weight, preferred_element_type=F32).astype(BF16) for h in hidden]
    produced = jnp.concatenate([p.reshape(-1, experts, part) for p in produced], axis=0)
    returned = expert_move(jnp.swapaxes(produced, 0, 1))

    mixed = lax.dot_general(
        placer,
        returned.reshape(experts * lines, part),
        (((0,), (0,)), ((), ())),
        preferred_element_type=F32,
    )
    mixed = (mixed[:tokens] + mixed[tokens:]).astype(BF16).reshape(chips, own, part)
    combined = chip_move(mixed)
    combined = jnp.swapaxes(combined, 0, 1).reshape(own, width)

    grad_rows = jnp.swapaxes(scaled, 0, 1).reshape(lines * experts, part)
    cut = early * held
    gradient = sum(
        lax.dot_general(h, g, (((0,), (0,)), ((), ())), preferred_element_type=F32)
        for h, g in zip(hidden, (grad_rows[:cut], grad_rows[cut:]))
    )
    kept = lax.dynamic_slice_in_dim(gradient, core * half, half, 1)
    given = lax.dynamic_slice_in_dim(gradient, (1 - core) * half, half, 1)
    gradient = kept + lax.ppermute(given, "dp", swap)
    return (combined, gradient[None])


def solution(mesh):
    in_specs = (
        P(("dp", "ctx", "tp"), None),
        P(("dp", "ctx", "tp"), None),
        P(("ctx", "tp"), "dp", None, None, None),
        P(("ctx", "tp"), None, "dp"),
        P(("dp", "ctx", "tp"), None),
    )
    out_specs = (P(("dp", "ctx", "tp"), None), P(("ctx", "tp"), None, "dp"))
    return jax.shard_map(layer, mesh=mesh, in_specs=in_specs, out_specs=out_specs, check_vma=False)
```

```python
import jax
import jax.numpy as jnp
from jax import lax
from jax.experimental import pallas as pl
from jax.experimental.layout import Layout, with_layout_constraint
from jax.sharding import PartitionSpec as P


CORES = 2
LANES = 128
F32 = jnp.float32
BF16 = jnp.bfloat16


def expert_move(buffer):
    return lax.all_to_all(buffer, ("ctx", "tp"), split_axis=0, concat_axis=0, tiled=True)


def parts_of(values, count):
    parts = []
    for _ in range(count):
        part = lax.reduce_precision(values, 8, 7)
        parts.append(part.astype(BF16))
        values = values - part
    return parts


def pack_kernel(routes_ref, gates_ref, grad_ref, out_ref):
    chips, own, length = out_ref.shape
    part = length - LANES
    gates = gates_ref[...]
    high = gates.astype(BF16)
    rest = gates - high.astype(F32)
    middle = rest.astype(BF16)
    low = (rest - middle.astype(F32)).astype(BF16)
    rows = [routes_ref[...].astype(F32), high.astype(F32), middle.astype(F32), low.astype(F32)]
    rows = jnp.concatenate(rows, axis=0)
    rows = jnp.concatenate([rows, jnp.zeros((LANES - rows.shape[0], own), F32)], axis=0)
    table = rows.T.astype(BF16)
    for chip in range(chips):
        out_ref[chip, :, :part] = grad_ref[:, chip * part : (chip + 1) * part]
        out_ref[chip, :, part:] = table


def placer_of(named, gates, experts, own, capacity, place_of):
    tokens = named.shape[0]
    groups = tokens // own
    shape = (experts, tokens)
    ids = lax.broadcasted_iota(jnp.int32, shape, 0).astype(F32)
    hit = named.T[:, None, :] == ids[None]
    names = jnp.any(hit, axis=0)
    gate_of = jnp.sum(jnp.where(hit, gates.T[:, None, :], 0.0), axis=0)
    at = lax.broadcasted_iota(jnp.int32, (tokens, tokens), 0)
    to = lax.broadcasted_iota(jnp.int32, (tokens, tokens), 1)
    earlier = jnp.logical_and(at // own == to // own, at < to).astype(BF16)
    rank = jnp.dot(names.astype(BF16), earlier, preferred_element_type=F32)
    group = place_of(lax.broadcasted_iota(jnp.int32, shape, 1) // own)
    code = jnp.where(names, group.astype(F32) * capacity + rank, -1.0)
    lines = capacity * groups
    place = code[:, None, :] == lax.broadcasted_iota(jnp.int32, (1, lines, tokens), 1).astype(F32)
    return jnp.concatenate(
        [jnp.where(place, p[:, None, :], jnp.zeros((), BF16)) for p in parts_of(gate_of, 2)], axis=2
    ).reshape(experts * lines, 2 * tokens)


def layer(routed_experts, route_gates, expert_hidden, down_weight, output_grad):
    dp = lax.axis_size("dp")
    chips = dp // CORES
    experts = lax.axis_size("ctx") * lax.axis_size("tp")
    own, topk = routed_experts.shape
    capacity, depth = expert_hidden.shape[3:]
    width = output_grad.shape[1]
    half = width // dp
    part = half * CORES
    tokens = chips * own
    lines = chips * capacity
    held = capacity * experts
    column = [[z * CORES + c for z in range(chips)] for c in range(CORES)]
    swap = [(d, d ^ 1) for d in range(dp)]
    core = lax.axis_index("dp") & 1
    chip = lax.axis_index("dp") // CORES

    def shift(block, by):
        moved = lax.ppermute(block, "dp", [(d, (d + CORES * by) % dp) for d in range(dp)])
        return with_layout_constraint(moved, Layout((0, 1)))

    def chip_move(blocks):
        return lax.all_to_all(
            blocks, "dp", split_axis=0, concat_axis=0, tiled=True, axis_index_groups=column
        )

    def in_order(group):
        ahead = (group + chips - chip) % chips
        return jnp.where(
            ahead > chips // 2, 2 * (chips - ahead), jnp.maximum(2 * ahead - 1, 0)
        )

    blocks = pl.pallas_call(
        pack_kernel,
        out_shape=jax.ShapeDtypeStruct((chips, own, part + LANES), BF16),
        name="pack_columns",
    )(routed_experts.T, route_gates.T, output_grad)
    arrived = chip_move(blocks)
    grads = arrived[:, :, :part].reshape(tokens, part)
    tables = arrived[:, :, part:].reshape(tokens, LANES).astype(F32)
    gates = sum(tables[:, topk * i : topk * (i + 1)] for i in (1, 2, 3))
    placer = placer_of(tables[:, :topk], gates, experts, own, capacity, in_order)
    outgoing = jnp.dot(placer, jnp.concatenate([grads, grads], axis=0), preferred_element_type=F32)
    outgoing = outgoing.astype(BF16).reshape(experts, lines, part)
    scaled = expert_move(outgoing)

    mine = jnp.swapaxes(expert_hidden[0, 0], 0, 1).reshape(held, depth)
    up = down = mine
    around = [mine]
    for _ in range(1, chips // 2):
        up, down = shift(up, 1), shift(down, -1)
        around += [down, up]
    last = [(d, (d + (CORES if d % CORES == 0 else -CORES)) % dp) for d in range(dp)]
    far = lax.ppermute(jnp.where(core == 0, up, down), "dp", last)
    around.append(with_layout_constraint(far, Layout((0, 1))))

    weight = down_weight[0]
    other = lax.ppermute(weight, "dp", swap)
    weight = jnp.concatenate(
        [jnp.where(core == 0, weight, other), jnp.where(core == 0, other, weight)], axis=1
    )
    weight = lax.optimization_barrier(weight)
    early = chips // 2 + 1
    hidden = [
        jnp.concatenate(blocks, axis=0)
        for blocks in (around[:early], around[early:])
    ]
    produced = [jnp.dot(h, weight, preferred_element_type=F32).astype(BF16) for h in hidden]
    produced = jnp.concatenate([p.reshape(-1, experts, part) for p in produced], axis=0)
    returned = expert_move(jnp.swapaxes(produced, 0, 1))

    mixed = lax.dot_general(
        placer,
        returned.reshape(experts * lines, part),
        (((0,), (0,)), ((), ())),
        preferred_element_type=F32,
    )
    mixed = (mixed[:tokens] + mixed[tokens:]).astype(BF16).reshape(chips, own, part)
    combined = chip_move(mixed)
    combined = jnp.swapaxes(combined, 0, 1).reshape(own, width)

    grad_rows = jnp.swapaxes(scaled, 0, 1).reshape(lines * experts, part)
    cut = early * held
    gradient = sum(
        lax.dot_general(h, g, (((0,), (0,)), ((), ())), preferred_element_type=F32)
        for h, g in zip(hidden, (grad_rows[:cut], grad_rows[cut:]))
    )
    kept = lax.dynamic_slice_in_dim(gradient, core * half, half, 1)
    given = lax.dynamic_slice_in_dim(gradient, (1 - core) * half, half, 1)
    gradient = kept + lax.ppermute(given, "dp", swap)
    return (combined, gradient[None])


def solution(mesh):
    in_specs = (
        P(("dp", "ctx", "tp"), None),
        P(("dp", "ctx", "tp"), None),
        P(("ctx", "tp"), "dp", None, None, None),
        P(("ctx", "tp"), None, "dp"),
        P(("dp", "ctx", "tp"), None),
    )
    out_specs = (P(("dp", "ctx", "tp"), None), P(("ctx", "tp"), None, "dp"))
    return jax.shard_map(layer, mesh=mesh, in_specs=in_specs, out_specs=out_specs, check_vma=False)
```
